32 devices in a mesh: dp: 2 (over x), ctx: 16 (over z, y, core).
Axes of the slice: x: 2, y: 2, z: 4, core: 2. Of those that a mesh axis runs over, the one named last changes fastest.
Arguments:
- features: bfloat16 [2, 2048, 1024], P('dp', 'ctx'), may hold values from -6 to 6
- gate_in: bfloat16 [2, 2048, 1024], P('dp', 'ctx'), may hold values from -6 to 6
- state_in: bfloat16 [2, 2048, 64], P('dp', 'ctx'), may hold values from -0.59765625 to 0.59765625
- state_out: bfloat16 [2, 2048, 64], P('dp', 'ctx'), may hold values from -0.59765625 to 0.59765625
- step_size: float32 [2, 8, 2048], P('dp', None, 'ctx'), may hold values from 0 to 4096
- decay_rate: float32 [8], replicated, may hold values from 0 to 1
- user_ids: int32 [2, 2048], P('dp', 'ctx'), may hold values from 0 to 3, never falling along the last dimension, each value on 1 to 1024 neighbouring positions
- norm_gain: bfloat16 [1024], replicated, may hold values from 0.099609375 to 1.8984375
- out_weight: bfloat16 [1024, 512], P(('dp', 'ctx')), may hold values from -0.1875 to 0.1875
- out_grad: bfloat16 [2, 2048, 512], P('dp', 'ctx'), may hold values from -6 to 6
Outputs:
- mixed: bfloat16 [2, 2048, 512], P('dp', 'ctx')
- feature_grad: bfloat16 [2, 2048, 1024], P('dp', 'ctx')
- weight_grad: float32 [1024, 512], P(('dp', 'ctx'))
The draws below stay inside these ranges and needn't reach their ends.
Inputs may be any that keep to these rules, and one draw needn't show every extreme that they name: `user_ids`: each of the 4 users of a history holds consecutive events; ids never fall along a history, and one user holds exactly 1024 events.
All inputs are finite; a program needn't handle non-finite values.
Results may differ from the reference program's by a relative error of at most 0.019.
Values may be sent and summed in bfloat16 or wider, within the bound.
A program may use at most 64 MiB of HBM per device.

```python
import math
import jax
import jax.numpy as jnp
import numpy as np
from jax import lax

DW = 512
HEADS = 8
NSTATE = 64
TOK_DEV = 128
INNER = 1024
PACKED_OCCASIONS = 2048
USERS = 4
N_DP = 2


def draw_step_size(key, part):
    identifier_seed, segment_lookup_entries, identifier_offset, spurt_identifier = jax.random.split(key, 4)
    entire_dimensions = (N_DP, HEADS, PACKED_OCCASIONS)
    baseline_tolerance = jnp.exp(jax.random.uniform(identifier_seed, entire_dimensions, jnp.float32, math.log(0.5), math.log(2.0)))
    block_scale = jnp.exp(jax.random.uniform(segment_lookup_entries, (N_DP, 1, PACKED_OCCASIONS // TOK_DEV), jnp.float32, math.log(0.4), math.log(2.5)))
    multiplier_value = jnp.repeat(block_scale, TOK_DEV, axis=2)
    spurt_offset = jax.random.randint(identifier_offset, (N_DP, 4, 1), 0, PACKED_OCCASIONS)
    token_offsets = jnp.arange(PACKED_OCCASIONS, dtype=jnp.int32)
    spurt_enabled = jnp.any(token_offsets[None, None, :] == spurt_offset, axis=1)[:, None, :]
    spurt_length = PACKED_OCCASIONS * jax.random.uniform(spurt_identifier, entire_dimensions, jnp.float32, 0.8, 2.0)
    return jnp.where(spurt_enabled, spurt_length, baseline_tolerance * multiplier_value)


def draw_decay_rate(key, part):
    key_order, key_slow, key_fast = jax.random.split(key, 3)
    ranking = jax.random.permutation(key_order, HEADS)
    forgetful = ranking < HEADS // 2
    slow_rate = jnp.exp(jax.random.uniform(key_slow, (HEADS,), jnp.float32, math.log(0.1), math.log(0.3))) / PACKED_OCCASIONS
    fast_rate = jnp.exp(jax.random.uniform(key_fast, (HEADS,), jnp.float32, math.log(0.015), math.log(0.04)))
    return jnp.where(forgetful, fast_rate, slow_rate)


def level_of(own_key, extent, cuts, low, top_value):
    def one(position, blocks):
        heights = jax.random.uniform(jax.random.fold_in(jax.random.fold_in(own_key, 6), position), (blocks,), jnp.float32, low / len(cuts), top_value / len(cuts))
        return jnp.repeat(jnp.exp(heights), extent[position] // blocks).reshape((-1,) + (1,) * (len(extent) - position - 1))

    factor_of = one(*cuts[0])
    for cut in cuts[1:]:
        factor_of = factor_of * one(*cut)
    return factor_of


def length_profile(number_of, total, most, skew):
    weights = [(1 << 20) // math.isqrt(rank ** skew) + 1 for rank in range(2, number_of + 1)]
    surplus, counts = total - most - (number_of - 1), [1] * (number_of - 1)
    while surplus > 0:
        candidates = [i for i in range(number_of - 1) if counts[i] < most]
        whole, budget = sum([weights[i] for i in candidates]), surplus
        for i in candidates:
            extra = min(most - counts[i], max(1, budget * weights[i] // whole), surplus)
            counts[i] = counts[i] + extra
            surplus = surplus - extra
    return np.array([most] + counts)


def uneven_parts(stream_key, count, total, reach, skew):
    if count == 2:
        one = jax.random.randint(stream_key, (), max(1, total - reach), min(reach, total - 1) + 1)
        return jnp.stack([one, total - one])
    lengths = jnp.asarray(length_profile(count, total, reach, skew), jnp.int32)
    twos = (count - 1) // 2
    donor, sink = lengths[1:1 + 2 * twos:2], lengths[2:2 + 2 * twos:2]
    slack = jnp.minimum(donor - 1, reach - sink)
    passed = jax.random.randint(jax.random.fold_in(stream_key, 1), (twos,), 0, 1 << 20) % (slack + 1)
    lengths = lengths.at[1:1 + 2 * twos:2].set(donor - passed).at[2:2 + 2 * twos:2].set(sink + passed)
    return lengths[jax.random.permutation(jax.random.fold_in(stream_key, 2), count)]


def centred(own_key, extent, scale, most, shards=(), kind=jnp.bfloat16):
    array = jax.random.normal(own_key, extent, jnp.float32) * scale
    if len(shards) > 0:
        array = level_of(own_key, extent, shards, -0.22, 0.18) * array
    return jnp.clip(array, min=-most, max=most).astype(kind)


def setup_inputs(seed: int = 0) -> dict:
    arg_keys = jax.random.split(jax.random.key(seed), 11)
    features = centred(arg_keys[0], (N_DP, PACKED_OCCASIONS, INNER), 1.0, 6.0, ((0, 2), (1, 16)))
    gate_in = centred(arg_keys[1], (N_DP, PACKED_OCCASIONS, INNER), 1.0, 6.0, ((0, 2), (1, 16)))
    state_in = centred(arg_keys[2], (N_DP, PACKED_OCCASIONS, NSTATE), 0.1, 0.59765625, ((0, 2), (1, 16)))
    state_out = centred(arg_keys[3], (N_DP, PACKED_OCCASIONS, NSTATE), 0.1, 0.59765625, ((0, 2), (1, 16)))
    step_size = draw_step_size(jax.random.fold_in(arg_keys[10], 71), 0)
    decay_rate = draw_decay_rate(jax.random.fold_in(arg_keys[10], 71), 0)
    user_ids = jax.vmap(lambda own: jnp.searchsorted(jnp.cumsum(uneven_parts(own, USERS, PACKED_OCCASIONS, PACKED_OCCASIONS // 2, 2)), jnp.arange(PACKED_OCCASIONS), side="right"))(jax.random.split(arg_keys[6], N_DP)).reshape((N_DP, PACKED_OCCASIONS)).astype(jnp.int32)
    norm_gain = jnp.clip(1.0 + 0.18 * jax.random.normal(arg_keys[7], (INNER,), jnp.float32), 0.099609375, 1.8984375).astype(jnp.bfloat16)
    out_weight = centred(arg_keys[8], (INNER, DW), INNER ** -0.5, 0.1875, ((0, 32),))
    out_grad = centred(arg_keys[9], (N_DP, PACKED_OCCASIONS, DW), 1.0, 6.0, ((0, 2), (1, 16)))
    return {"features": features, "gate_in": gate_in, "state_in": state_in, "state_out": state_out, "step_size": step_size, "decay_rate": decay_rate, "user_ids": user_ids, "norm_gain": norm_gain, "out_weight": out_weight, "out_grad": out_grad}


eps = 1e-05
highest = lax.Precision.HIGHEST

def block_terms(values, keys_in, reads, logdec, user_row, before_user, after_user):
    row_count = values.shape[0]
    head_count = logdec.shape[0]
    cumulative = jnp.cumsum(logdec, axis=1)
    total_log = cumulative[:, -1]
    intersections = jnp.dot(reads, keys_in.T, preferred_element_type=jnp.float32)
    same_user = user_row[:, None] == user_row[None, :]
    spread = cumulative[:, :, None] - cumulative[:, None, :]
    doubled = 1.0 + jnp.eye(row_count, dtype=jnp.float32)
    weights = jnp.where(same_user[None], intersections[None] * doubled[None] * jnp.exp(-jnp.abs(spread)), 0.0).astype(jnp.bfloat16)
    per_head = values.reshape(row_count, head_count, -1)
    inner = jnp.einsum('hts,shp->thp', weights.astype(jnp.float32), per_head.astype(jnp.float32), precision=highest)
    tail_user = (user_row == user_row[-1]).astype(jnp.float32)
    head_user = (user_row == user_row[0]).astype(jnp.float32)
    fwd_scale = (jnp.exp(total_log[:, None] - cumulative) * tail_user[None]).T
    rev_scale = (jnp.exp(cumulative) * head_user[None]).T
    fwd_keys = (keys_in[:, None, :] * fwd_scale[:, :, None]).astype(jnp.bfloat16)
    rev_keys = (keys_in[:, None, :] * rev_scale[:, :, None]).astype(jnp.bfloat16)
    fwd_state = jnp.einsum('shn,shp->hnp', fwd_keys.astype(jnp.float32), per_head.astype(jnp.float32), precision=highest).astype(jnp.bfloat16)
    rev_state = jnp.einsum('shn,shp->hnp', rev_keys.astype(jnp.float32), per_head.astype(jnp.float32), precision=highest).astype(jnp.bfloat16)
    passing = jnp.exp(total_log)
    fwd_gain = (passing * (user_row[-1] == before_user).astype(jnp.float32)).astype(jnp.bfloat16)
    rev_gain = (passing * (user_row[0] == after_user).astype(jnp.float32)).astype(jnp.bfloat16)
    return (inner, cumulative, fwd_gain, fwd_state, rev_gain, rev_state)

def apply_carries(inner, reads, cumulative, user_row, before_user, after_user, from_before, from_after):
    reads_wide = reads.astype(jnp.float32)
    earlier_part = jnp.einsum('tn,hnp->thp', reads_wide, from_before.astype(jnp.float32), precision=highest)
    following_part = jnp.einsum('tn,hnp->thp', reads_wide, from_after.astype(jnp.float32), precision=highest)
    earlier_scale = (jnp.exp(cumulative) * (user_row == before_user).astype(jnp.float32)[None]).T[:, :, None]
    following_scale = (jnp.exp(cumulative[:, -1:] - cumulative) * (user_row == after_user).astype(jnp.float32)[None]).T[:, :, None]
    row_count = inner.shape[0]
    return (inner + earlier_scale * earlier_part + following_scale * following_part).reshape(row_count, -1)

def block_terms_packed(packed):
    return block_terms(*packed)

def apply_packed(packed):
    return apply_carries(*packed)

def advance(running, pair):
    gain_now, state_now = pair
    following = (gain_now.astype(jnp.float32)[:, None, None] * running.astype(jnp.float32) + state_now.astype(jnp.float32)).astype(jnp.bfloat16)
    return (following, running)

def mix(values, keys_in, reads, logdec, user_row):
    block_count = PACKED_OCCASIONS // TOK_DEV
    head_count = logdec.shape[0]
    value_blocks = values.reshape(block_count, TOK_DEV, -1)
    key_blocks = keys_in.reshape(block_count, TOK_DEV, -1)
    read_blocks = reads.reshape(block_count, TOK_DEV, -1)
    log_blocks = logdec.reshape(head_count, block_count, TOK_DEV).transpose(1, 0, 2)
    user_blocks = user_row.reshape(block_count, TOK_DEV)
    padding = jnp.full((1,), -1, jnp.int32)
    before_all = jnp.concatenate([padding, user_blocks[:-1, -1].astype(jnp.int32)])
    after_all = jnp.concatenate([user_blocks[1:, 0].astype(jnp.int32), padding])
    inner, cumulative, fwd_gain, fwd_state, rev_gain, rev_state = lax.map(block_terms_packed, (value_blocks, key_blocks, read_blocks, log_blocks, user_blocks, before_all, after_all))
    empty_state = jnp.zeros(fwd_state.shape[1:], jnp.bfloat16)
    unused_one, from_before = lax.scan(advance, empty_state, (fwd_gain, fwd_state))
    unused_two, from_after = lax.scan(advance, empty_state, (rev_gain, rev_state), reverse=True)
    combined = lax.map(apply_packed, (inner, read_blocks, cumulative, user_blocks, before_all, after_all, from_before, from_after))
    return combined.reshape(PACKED_OCCASIONS, -1)

def reference(features, gate_in, state_in, state_out, step_size, decay_rate, user_ids, norm_gain, out_weight, out_grad):

    def one_sequence(sequence_in):
        values, gates, keys_in, reads, step_row, user_row, grad_local = sequence_in
        logdec = -step_row * decay_rate[:, None]
        mixed_wide = mix(values, keys_in, reads, logdec, user_row)

        def normalize(mixed_rows):
            gated = mixed_rows * jax.nn.silu(gates.astype(jnp.float32))
            multiplier_value = lax.rsqrt(lax.optimization_barrier(jnp.mean(gated * gated, axis=-1, keepdims=True)) + eps)
            return gated * multiplier_value * norm_gain.astype(jnp.float32)
        normed_wide, pullback = jax.vjp(normalize, mixed_wide)
        normed_out = normed_wide.astype(jnp.bfloat16)
        result = jnp.dot(normed_out, out_weight, preferred_element_type=jnp.float32).astype(jnp.bfloat16)
        grad_normed = lax.dot_general(grad_local, out_weight, (((1,), (1,)), ((), ())), preferred_element_type=jnp.float32)
        grad_mixed = pullback(grad_normed)[0].astype(jnp.bfloat16)
        grad_feat = mix(grad_mixed, reads, keys_in, logdec, user_row).astype(jnp.bfloat16)
        return (result, grad_feat, normed_out)
    mixed, feature_grad, normalized = lax.map(one_sequence, (features, gate_in, state_in, state_out, step_size, user_ids, out_grad))
    weight_grad = lax.dot_general(normalized.reshape(-1, INNER), out_grad.reshape(-1, DW), (((0,), (0,)), ((), ())), preferred_element_type=jnp.float32)
    return (mixed, feature_grad, weight_grad)
```

```python
import functools

import jax
import jax.numpy as jnp
from jax import lax
from jax.experimental import pallas as pl
from jax.experimental.pallas import tpu as pltpu
from jax.sharding import PartitionSpec as P

eps = 1e-05
MESH = pl.DeviceIdType.MESH
f32 = jnp.float32
bf16 = jnp.bfloat16
AUX = 16


def matmul(a, b, ca, cb, precision=None):
    return lax.dot_general(
        a, b, (((ca,), (cb,)), ((), ())), preferred_element_type=f32, precision=precision
    )


def kernel(
    dp,
    n,
    fused,
    feat,
    gate,
    state_in,
    state_out,
    step,
    rate,
    users,
    norm_gain,
    weight,
    out_grad,
    mixed,
    feature_grad,
    weight_grad,
    scratch,
):
    me = lax.axis_index("ctx")
    x = lax.axis_index("dp")
    tokens, inner_dim = feat.shape
    heads = step.shape[0]
    width = inner_dim // heads
    nstate = state_in.shape[1]
    share = 2 * heads * nstate // n
    half = n // 2

    barrier = pltpu.get_barrier_semaphore()

    def greet(k, _):
        pl.semaphore_signal(
            barrier, inc=1, device_id={"ctx": lax.rem(me + k, n)}, device_id_type=MESH
        )
        return 0

    lax.fori_loop(1, n, greet, 0)
    if fused:
        pl.semaphore_signal(barrier, inc=1, device_id={"dp": 1 - x}, device_id_type=MESH)
    pl.semaphore_wait(barrier, n - 1 + (1 if fused else 0))

    if fused:
        count_a = n // 4
        a, b, c = me // 4, (me // 2) % 2, me % 2
        y_peer = {"ctx": a * 4 + (1 - b) * 2 + c}
        x_peer = {"dp": 1 - x}
        core_peer = {"ctx": a * 4 + b * 2 + (1 - c)}
        full, wss, wrs = scratch["full"], scratch["wss"], scratch["wrs"]
        full[x, a, b, c] = weight[...]

        def z_copy(source, slot, to):
            return pltpu.make_async_remote_copy(
                src_ref=weight,
                dst_ref=full.at[x, source, b, c],
                send_sem=wss.at[slot],
                recv_sem=wrs.at[source],
                device_id={"ctx": to * 4 + b * 2 + c},
                device_id_type=MESH,
            )

        def w_copy(view, slot, peer):
            return pltpu.make_async_remote_copy(
                src_ref=view,
                dst_ref=view,
                send_sem=wss.at[count_a + slot],
                recv_sem=wrs.at[count_a + slot],
                device_id=peer,
                device_id_type=MESH,
            )

        for k in range(1, count_a):
            z_copy(a, k, lax.rem(a + k, count_a)).start()
        sent_y = w_copy(full.at[x, :, b, c], 0, y_peer)
        got_y = w_copy(full.at[x, :, 1 - b, c], 0, y_peer)
        sent_x = w_copy(full.at[x, :, :, c], 1, x_peer)
        got_x = w_copy(full.at[1 - x, :, :, c], 1, x_peer)
        sent_core = w_copy(full.at[:, :, :, c], 2, core_peer)
        got_core = w_copy(full.at[:, :, :, 1 - c], 2, core_peer)

    row_of = lax.broadcasted_iota(jnp.int32, (tokens, tokens), 0)
    column_of = lax.broadcasted_iota(jnp.int32, (tokens, tokens), 1)
    head_of = lax.broadcasted_iota(jnp.int32, (heads, 1), 0)
    rates = jnp.zeros((heads, 1), f32)
    for h in range(heads):
        rates = jnp.where(head_of == h, rate[h], rates)
    logdec = -step[...] * rates
    upto = (row_of <= column_of).astype(f32)
    cumulative = matmul(logdec, upto, 1, 0, lax.Precision.HIGHEST)
    user_row = users[...].astype(f32)
    stacked = jnp.concatenate(
        [
            cumulative,
            jnp.broadcast_to(user_row, (8, tokens)),
            jnp.zeros((tokens - heads - 8, tokens), f32),
        ],
        axis=0,
    )
    turned = stacked.T
    along = turned[:, :heads]
    user_col = turned[:, heads : heads + 1]
    total = along[tokens - 1 : tokens, :]
    first_user = user_col[0:1, :]
    last_user = user_col[tokens - 1 : tokens, :]
    to_end = jnp.exp(total - along)
    from_start = jnp.exp(along)
    fwd_scale = jnp.where(user_col == last_user, to_end, 0.0)
    rev_scale = jnp.where(user_col == first_user, from_start, 0.0)
    passing = jnp.exp(total)
    aux_row = lax.broadcasted_iota(jnp.int32, (AUX, width), 0)

    def send_states(which, values, keys):
        st, ra = scratch["st"].at[which], scratch["ra"].at[which]
        keys_wide = keys[...].astype(f32)
        for h in range(heads):
            v = values[:, h * width : (h + 1) * width]
            both = jnp.concatenate(
                [
                    (keys_wide * fwd_scale[:, h : h + 1]).astype(bf16),
                    (keys_wide * rev_scale[:, h : h + 1]).astype(bf16),
                ],
                axis=1,
            )
            states = matmul(both, v, 0, 0).astype(bf16)
            for d in range(2):
                aux = jnp.where(
                    aux_row == 0, passing[:, h : h + 1], last_user if d == 0 else first_user
                ).astype(bf16)
                for q in range(nstate // share):
                    unit = (d * heads + h) * (nstate // share) + q
                    start = d * nstate + q * share
                    st[unit, 0:share, :] = states[start : start + share]
                    st[unit, share : share + AUX, :] = aux

        def send(k, _):
            to = lax.rem(me + k, n)
            pltpu.make_async_remote_copy(
                src_ref=st.at[to],
                dst_ref=ra.at[me],
                send_sem=scratch["a_send"].at[which, to],
                recv_sem=scratch["a_recv"].at[which, me],
                device_id={"ctx": to},
                device_id_type=MESH,
            ).start()
            return 0

        lax.fori_loop(1, n, send, 0)
        ra[me] = st[me]

    def arrival(name, which, ref_from, ref_to, j):
        return pltpu.make_async_remote_copy(
            src_ref=ref_from.at[j],
            dst_ref=ref_to.at[j],
            send_sem=scratch[name + "_send"].at[which, j],
            recv_sem=scratch[name + "_recv"].at[which, j],
            device_id={"ctx": j},
            device_id_type=MESH,
        )

    def scan_states(which):
        st, ra = scratch["st"].at[which], scratch["ra"].at[which]
        sb, rb = scratch["sb"].at[which], scratch["rb"].at[which]
        backward = me // half

        def body(p, carry):
            running, previous = carry
            j = p + backward * (n - 1 - 2 * p)

            @pl.when(j != me)
            def _():
                arrival("a", which, st, ra, j).wait_recv()

            sb[j, 0:share, :] = running.astype(bf16)
            sb[j, share : share + AUX, :] = jnp.broadcast_to(previous, (AUX, width)).astype(bf16)

            @pl.when(j != me)
            def _():
                pltpu.make_async_remote_copy(
                    src_ref=sb.at[j],
                    dst_ref=rb.at[me],
                    send_sem=scratch["b_send"].at[which, j],
                    recv_sem=scratch["b_recv"].at[which, me],
                    device_id={"ctx": j},
                    device_id_type=MESH,
                ).start()

            block = ra[j].astype(f32)
            boundary = block[share + 1 : share + 2]
            gain = jnp.where(boundary == previous, block[share : share + 1], 0.0)
            running = (gain * running + block[0:share]).astype(bf16).astype(f32)
            return running, boundary

        lax.fori_loop(
            0, n, body, (jnp.zeros((share, width), f32), jnp.full((1, width), -1.0, f32))
        )
        rb[me] = sb[me]

    def wait_carries(which):
        sb, rb = scratch["sb"].at[which], scratch["rb"].at[which]

        def body(k, _):
            arrival("b", which, sb, rb, lax.rem(me + k, n)).wait_recv()
            return 0

        lax.fori_loop(1, n, body, 0)

    def finish_sends(which):
        st, ra = scratch["st"].at[which], scratch["ra"].at[which]
        sb, rb = scratch["sb"].at[which], scratch["rb"].at[which]

        def body(k, _):
            j = lax.rem(me + k, n)
            arrival("a", which, st, ra, j).wait_send()
            arrival("b", which, sb, rb, j).wait_send()
            return 0

        lax.fori_loop(1, n, body, 0)

    def apply_carries(which, reads, h):
        rb = scratch["rb"].at[which]
        pieces = nstate // share
        before_user = rb[0, share : share + 1, 0:1].astype(f32)
        after_user = rb[n - 1, share : share + 1, 0:1].astype(f32)
        early = jnp.where(user_col == before_user, from_start[:, h : h + 1], 0.0)
        late = jnp.where(user_col == after_user, to_end[:, h : h + 1], 0.0)
        parts = []
        for d in range(2):
            base = (d * heads + h) * pieces
            if pieces == 1:
                state = rb[base, 0:share, :]
            else:
                state = jnp.concatenate([rb[base + q, 0:share, :] for q in range(pieces)], axis=0)
            parts.append(matmul(reads[...], state, 1, 0))
        return early * parts[0] + late * parts[1]

    send_states(0, feat, state_in)
    if fused:
        for k in range(1, count_a):
            source = lax.rem(a + k, count_a)
            z_copy(source, k, a).wait_recv()
        sent_y.start()

    scores = matmul(state_out[...], state_in[...], 1, 1)
    scores = jnp.where(row_of == column_of, 2.0 * scores, scores)
    scores = jnp.where(user_col == user_row, scores, 0.0)
    mixw, y = scratch["mixw"], scratch["y"]
    for h in range(heads):
        spread = jnp.abs(along[:, h : h + 1] - cumulative[h : h + 1, :])
        weights = (scores * jnp.exp(-spread)).astype(bf16)
        mixw[h] = weights
        cols = slice(h * width, (h + 1) * width)
        y[:, cols] = matmul(weights, feat[:, cols], 1, 0)
    if fused:
        got_y.wait_recv()
        sent_x.start()
    silu, cot, normed, grad_mixed = (
        scratch["silu"],
        scratch["cot"],
        scratch["normed"],
        scratch["grad_mixed"],
    )
    gates = gate[...].astype(f32)
    silu[...] = gates / (1.0 + jnp.exp(-gates))
    scan_states(0)
    if fused:
        got_x.wait_recv()
        sent_core.start()
        got_core.wait_recv()
        whole = full[...].reshape(inner_dim, weight.shape[1])
    else:
        whole = weight[...]
    scale = norm_gain[...].astype(f32)
    cot[...] = matmul(out_grad[...], whole, 1, 1) * scale
    wait_carries(0)
    for h in range(heads):
        cols = slice(h * width, (h + 1) * width)
        y[:, cols] = (y[:, cols] + apply_carries(0, state_out, h)) * silu[:, cols]
    gated = y[...]
    multiplier = lax.rsqrt(jnp.mean(gated * gated, axis=1, keepdims=True) + eps)
    back = cot[...]
    slope = jnp.mean(back * gated, axis=1, keepdims=True) * multiplier * multiplier
    grad_mixed[...] = ((back - gated * slope) * multiplier * silu[...]).astype(bf16)
    send_states(1, grad_mixed, state_out)

    normed[...] = (y[...] * multiplier * scale).astype(bf16)
    if fused:
        part = scratch["part"]
        rss, rrs = scratch["rss"], scratch["rrs"]
        rows = weight.shape[0]
        part[...] = matmul(normed[...], out_grad[...], 0, 0).astype(bf16).reshape(part.shape)

        def r_copy(source, target, slot, peer):
            return pltpu.make_async_remote_copy(
                src_ref=source,
                dst_ref=target,
                send_sem=rss.at[slot],
                recv_sem=rrs.at[slot],
                device_id=peer,
                device_id_type=MESH,
            )

        one, two, three, four = (scratch[name] for name in ("one", "two", "three", "four"))
        r_core = r_copy(part.at[:, :, :, 1 - c], one, count_a, core_peer)
        r_x = r_copy(one.at[1 - x], two, count_a + 1, x_peer)
        r_y = r_copy(two.at[:, 1 - b], three, count_a + 2, y_peer)
        r_core.start()
    else:
        weight_grad[...] = matmul(normed[...], out_grad[...], 0, 0)

    for h in range(heads):
        cols = slice(h * width, (h + 1) * width)
        y[:, cols] = matmul(mixw[h], grad_mixed[:, cols], 0, 0)
    if fused:
        r_core.wait_recv()
        one[...] = (one[...].astype(f32) + part[:, :, :, c].astype(f32)).astype(bf16)
        r_x.start()
    scan_states(1)
    mixed[...] = matmul(normed[...], whole, 1, 0).astype(bf16)
    if fused:
        r_x.wait_recv()
        two[...] = (two[...].astype(f32) + one[x].astype(f32)).astype(bf16)
        r_y.start()
    wait_carries(1)
    for h in range(heads):
        cols = slice(h * width, (h + 1) * width)
        feature_grad[:, cols] = (y[:, cols] + apply_carries(1, state_in, h)).astype(bf16)
    if fused:
        r_y.wait_recv()
        three[...] = (three[...].astype(f32) + two[:, b].astype(f32)).astype(bf16)

        def last_copy(k, source, target, to):
            return pltpu.make_async_remote_copy(
                src_ref=three.at[source],
                dst_ref=four.at[target],
                send_sem=rss.at[k],
                recv_sem=rrs.at[target],
                device_id={"ctx": to * 4 + b * 2 + c},
                device_id_type=MESH,
            )

        for k in range(1, count_a):
            to = lax.rem(a + k, count_a)
            last_copy(k, to, a, to).start()
        result = three[a].astype(f32)
        for k in range(1, count_a):
            source = lax.rem(a + k, count_a)
            last_copy(k, source, source, source).wait_recv()
            result = result + four[source].astype(f32)
        weight_grad[...] = result
        for k in range(1, count_a):
            to = lax.rem(a + k, count_a)
            last_copy(k, to, a, to).wait_send()
            z_copy(a, k, to).wait_send()
        for copy in (sent_y, sent_x, sent_core, r_core, r_x, r_y):
            copy.wait_send()
    finish_sends(0)
    finish_sends(1)


def local(
    dp,
    n,
    features,
    gate_in,
    state_in,
    state_out,
    step_size,
    decay_rate,
    user_ids,
    norm_gain,
    out_weight,
    out_grad,
):
    tokens, inner_dim = features.shape[1:]
    heads = step_size.shape[1]
    width = inner_dim // heads
    nstate = state_in.shape[2]
    rows, out_dim = out_weight.shape
    fused = dp == 2 and n == 16 and rows % 16 == 0
    share = 2 * heads * nstate // n
    states = pltpu.VMEM((2, n, share + AUX, width), bf16)
    dma = pltpu.SemaphoreType.DMA
    scratch = dict(
        st=states,
        ra=states,
        sb=states,
        rb=states,
        a_send=dma((2, n)),
        a_recv=dma((2, n)),
        b_send=dma((2, n)),
        b_recv=dma((2, n)),
        mixw=pltpu.VMEM((heads, tokens, tokens), bf16),
        y=pltpu.VMEM((tokens, inner_dim), f32),
        silu=pltpu.VMEM((tokens, inner_dim), f32),
        cot=pltpu.VMEM((tokens, inner_dim), f32),
        normed=pltpu.VMEM((tokens, inner_dim), bf16),
        grad_mixed=pltpu.VMEM((tokens, inner_dim), bf16),
    )
    if fused:
        count_a = n // 4
        sems = dma((count_a + 3,))
        scratch.update(
            full=pltpu.VMEM((2, count_a, 2, 2, rows, out_dim), bf16),
            part=pltpu.VMEM((2, count_a, 2, 2, rows, out_dim), bf16),
            one=pltpu.VMEM((2, count_a, 2, rows, out_dim), bf16),
            two=pltpu.VMEM((count_a, 2, rows, out_dim), bf16),
            three=pltpu.VMEM((count_a, rows, out_dim), bf16),
            four=pltpu.VMEM((count_a, rows, out_dim), bf16),
            wss=sems,
            wrs=sems,
            rss=sems,
            rrs=sems,
        )
        held = out_weight
    else:
        held = lax.all_gather(out_weight, ("dp", "ctx"), axis=0, tiled=True)
    names = list(scratch)

    def body(*refs):
        kernel(dp, n, fused, *refs[:13], dict(zip(names, refs[13:])))

    vmem = pl.BlockSpec(memory_space=pltpu.VMEM)
    mixed, feature_grad, weight_grad = pl.pallas_call(
        body,
        out_shape=(
            jax.ShapeDtypeStruct((tokens, out_dim), bf16),
            jax.ShapeDtypeStruct((tokens, inner_dim), bf16),
            jax.ShapeDtypeStruct(held.shape, f32),
        ),
        in_specs=[vmem] * 5 + [pl.BlockSpec(memory_space=pltpu.SMEM)] + [vmem] * 4,
        out_specs=(vmem, vmem, vmem),
        scratch_shapes=list(scratch.values()),
        compiler_params=pltpu.CompilerParams(
            collective_id=0, has_side_effects=True, vmem_limit_bytes=40 << 20
        ),
        name="mixer",
    )(
        features[0],
        gate_in[0],
        state_in[0],
        state_out[0],
        step_size[0],
        decay_rate,
        user_ids,
        norm_gain.reshape(1, -1),
        held,
        out_grad[0],
    )
    if not fused:
        weight_grad = lax.psum_scatter(
            weight_grad, ("dp", "ctx"), scatter_dimension=0, tiled=True
        )
    return mixed[None], feature_grad[None], weight_grad


def solution(mesh):
    placed = (
        P("dp", "ctx", None),
        P("dp", "ctx", None),
        P("dp", "ctx", None),
        P("dp", "ctx", None),
        P("dp", None, "ctx"),
        P(),
        P("dp", "ctx"),
        P(),
        P(("dp", "ctx"), None),
        P("dp", "ctx", None),
    )
    return jax.shard_map(
        functools.partial(local, mesh.shape["dp"], mesh.shape["ctx"]),
        mesh=mesh,
        in_specs=placed,
        out_specs=(P("dp", "ctx", None), P("dp", "ctx", None), P(("dp", "ctx"), None)),
        check_vma=False,
    )
```

```python
import functools

import jax
import jax.numpy as jnp
from jax import lax
from jax.experimental import pallas as pl
from jax.experimental.pallas import tpu as pltpu
from jax.sharding import PartitionSpec as P

eps = 1e-05
MESH = pl.DeviceIdType.MESH
f32 = jnp.float32
bf16 = jnp.bfloat16
AUX = 16


def matmul(a, b, ca, cb, precision=None):
    return lax.dot_general(
        a, b, (((ca,), (cb,)), ((), ())), preferred_element_type=f32, precision=precision
    )


def kernel(
    n,
    fused,
    feat_hbm,
    gate_hbm,
    keys_t,
    reads_t,
    step,
    rate,
    users,
    norm_gain,
    weight_hbm,
    out_grad_hbm,
    mixed,
    feature_grad,
    weight_grad,
    scratch,
):
    me = lax.axis_index("ctx")
    x = lax.axis_index("dp")
    chips = n // 2
    chip, c = me // 2, me % 2
    feat, gate, out_grad = scratch["feat"], scratch["gate"], scratch["out_grad"]
    tokens, inner_dim = feat.shape
    heads = step.shape[0]
    width = inner_dim // heads
    nstate = keys_t.shape[0]
    share = 2 * heads * nstate // n
    pieces = nstate // share
    core_peer = {"ctx": chip * 2 + 1 - c}
    loads = scratch["loads"]

    def signal(to):
        pl.semaphore_signal(barrier, inc=1, device_id=to, device_id_type=MESH)

    def remote(source, target, send_sem, recv_sem, to):
        return pltpu.make_async_remote_copy(
            src_ref=source,
            dst_ref=target,
            send_sem=send_sem,
            recv_sem=recv_sem,
            device_id=to,
            device_id_type=MESH,
        )

    get_feat = pltpu.make_async_copy(feat_hbm, feat, loads.at[0])
    get_gate = pltpu.make_async_copy(gate_hbm, gate, loads.at[1])
    get_grad = pltpu.make_async_copy(out_grad_hbm, out_grad, loads.at[2])
    if fused:
        count_a = n // 4
        a, b = me // 4, (me // 2) % 2
        full, wss, wrs = scratch["full"], scratch["wss"], scratch["wrs"]
        rows, out_dim = weight_hbm.shape
        get_weight = pltpu.make_async_copy(weight_hbm, full.at[x, a, b, c], loads.at[3])
    else:
        get_weight = pltpu.make_async_copy(weight_hbm, scratch["full"], loads.at[3])
    get_weight.start()
    get_feat.start()
    get_grad.start()
    get_gate.start()

    barrier = pltpu.get_barrier_semaphore()

    def greet(k, _):
        signal({"ctx": lax.rem(chip + k, chips) * 2 + c})
        return 0

    lax.fori_loop(1, chips, greet, 0)
    signal(core_peer)
    if fused:
        signal({"dp": 1 - x})
    pl.semaphore_wait(barrier, chips + (1 if fused else 0))

    if fused:
        get_weight.wait()
        fx = x + c * (1 - 2 * x)
        fb = b + (1 - c) * (1 - 2 * b)
        y_peer = {"dp": x, "ctx": a * 4 + (1 - b) * 2 + c}
        x_peer = {"dp": 1 - x, "ctx": me}
        first_peer = {
            "dp": 1 - fx,
            "ctx": a * 4 + (1 - fb) * 2 + c,
        }
        second_peer = {"dp": fx, "ctx": a * 4 + fb * 2 + c}

        def z_copy(source, slot, to):
            view = full.at[x, source, b, c]
            return remote(
                view, view, wss.at[slot], wrs.at[source], {"ctx": to * 4 + b * 2 + c}
            )

        def w_copy(view, slot, peer):
            return remote(view, view, wss.at[count_a + slot], wrs.at[count_a + slot], peer)

        for k in range(1, count_a):
            z_copy(a, k, lax.rem(a + k, count_a)).start()
        w_y = w_copy(full.at[x, :, b, c], 0, y_peer)
        w_x = w_copy(full.at[x, :, b, c], 1, x_peer)
        w_on = w_copy(full.at[fx, :, fb, c], 2, first_peer)
        w_core = w_copy(full.at[:, :, :, c], 3, core_peer)

    row_of = lax.broadcasted_iota(jnp.int32, (tokens, tokens), 0)
    column_of = lax.broadcasted_iota(jnp.int32, (tokens, tokens), 1)
    head_of = lax.broadcasted_iota(jnp.int32, (heads, 1), 0)
    rates = jnp.zeros((heads, 1), f32)
    for h in range(heads):
        rates = jnp.where(head_of == h, rate[h], rates)
    logdec = -step[...] * rates
    upto = (row_of <= column_of).astype(f32)
    cumulative = matmul(logdec, upto, 1, 0, lax.Precision.HIGHEST)
    total = cumulative[:, tokens - 1 : tokens]
    user_row = users[...].astype(f32)
    first_user = user_row[:, 0:1]
    last_user = user_row[:, tokens - 1 : tokens]
    from_start = jnp.exp(cumulative)
    to_end = jnp.exp(total - cumulative)
    passing = jnp.exp(total)
    fwd_scale = jnp.where(user_row == last_user, to_end, 0.0)
    rev_scale = jnp.where(user_row == first_user, from_start, 0.0)
    stacked = jnp.concatenate(
        [
            cumulative,
            from_start,
            to_end,
            jnp.broadcast_to(user_row, (8, tokens)),
            jnp.zeros((tokens - 3 * heads - 8, tokens), f32),
        ],
        axis=0,
    ).T
    along = stacked[:, 0:heads]
    start_col = stacked[:, heads : 2 * heads]
    end_col = stacked[:, 2 * heads : 3 * heads]
    user_col = stacked[:, 3 * heads : 3 * heads + 1]
    own_col = jnp.where(c == 1, start_col, end_col)
    other_col = jnp.where(c == 1, end_col, start_col)
    aux_row = lax.broadcasted_iota(jnp.int32, (AUX, width), 0)

    def chip_copy(name, which, source, target, index, slot, to):
        return remote(
            source.at[index],
            target.at[slot],
            scratch[name + "_send"].at[which, to],
            scratch[name + "_recv"].at[which, slot],
            {"ctx": to * 2 + c},
        )

    def refs(which):
        return [scratch[name].at[which] for name in ("st", "pt", "ct", "ra", "sb", "rb", "rx")]

    def pair_copy(which):
        st, pt = refs(which)[:2]
        return remote(
            st.at[c], pt, scratch["p_send"].at[which], scratch["p_recv"].at[which], core_peer
        )

    def relay_copy(which, u):
        rb, rx = refs(which)[5:]
        return remote(
            rb.at[u],
            rx.at[u],
            scratch["x_send"].at[which, u],
            scratch["x_recv"].at[which, u],
            core_peer,
        )

    def make_states(which, values, keys):
        st = refs(which)[0]
        wide = keys[...].astype(f32)
        for h in range(heads):
            v = values[:, h * width : (h + 1) * width]
            both = jnp.concatenate(
                [wide * fwd_scale[h : h + 1, :], wide * rev_scale[h : h + 1, :]], axis=0
            ).astype(bf16)
            states = matmul(both, v, 1, 0).astype(bf16)
            for d in range(2):
                aux = jnp.where(
                    aux_row == 0, passing[h : h + 1, :], last_user if d == 0 else first_user
                ).astype(bf16)
                for q in range(pieces):
                    start = d * nstate + q * share
                    st[d, h * pieces + q, 0:share, :] = states[start : start + share]
                    st[d, h * pieces + q, share : share + AUX, :] = aux
        pair_copy(which).start()

    def send_chip(which):
        st, pt, ct, ra, sb, rb, rx = refs(which)
        pair_copy(which).wait_recv()
        mine, theirs = st[1 - c].astype(f32), pt[...].astype(f32)
        gain = mine[:, share : share + 1]
        same = mine[:, share + 1 : share + 2] == theirs[:, share + 1 : share + 2]
        ct[:, 0:share, :] = (
            jnp.where(same, gain, 0.0) * theirs[:, 0:share] + mine[:, 0:share]
        ).astype(bf16)
        ct[:, share : share + AUX, :] = jnp.where(
            aux_row[None] == 0, mine[:, share:] * theirs[:, share:], mine[:, share:]
        ).astype(bf16)

        def send(k, _):
            to = lax.rem(chip + k, chips)
            chip_copy("a", which, ct, ra, to, chip, to).start()
            return 0

        lax.fori_loop(1, chips, send, 0)
        ra[chip] = ct[chip]

    def scan_states(which):
        st, pt, ct, ra, sb, rb, rx = refs(which)

        def body(p, carry):
            running, previous = carry
            j = p + (1 - c) * (chips - 1 - 2 * p)

            @pl.when(j != chip)
            def _():
                chip_copy("a", which, ct, ra, j, j, j).wait_recv()

            sb[j, 0:share, :] = running.astype(bf16)
            sb[j, share : share + AUX, :] = jnp.broadcast_to(previous, (AUX, width)).astype(bf16)

            @pl.when(j != chip)
            def _():
                chip_copy("b", which, sb, rb, j, chip, j).start()

            block = ra[j].astype(f32)
            boundary = block[share + 1 : share + 2]
            gain = jnp.where(boundary == previous, block[share : share + 1], 0.0)
            running = (gain * running + block[0:share]).astype(bf16).astype(f32)
            return running, boundary

        lax.fori_loop(
            0, chips, body, (jnp.zeros((share, width), f32), jnp.full((1, width), -1.0, f32))
        )
        rb[chip] = sb[chip]
        relay_copy(which, chip).start()

    def relay(which):
        st, pt, ct, ra, sb, rb, rx = refs(which)

        def body(k, _):
            u = lax.rem(chip + k, chips)
            chip_copy("b", which, sb, rb, u, u, u).wait_recv()
            relay_copy(which, u).start()
            return 0

        lax.fori_loop(1, chips, body, 0)
        theirs, past = pt[...].astype(f32), rb[...].astype(f32)
        same = theirs[:, share + 1 : share + 2] == past[:, share + 1 : share + 2]
        scratch["oc"][...] = (
            jnp.where(same, theirs[:, share : share + 1], 0.0) * past[:, 0:share]
            + theirs[:, 0:share]
        ).astype(bf16)

        def arrive(u, _):
            relay_copy(which, u).wait_recv()
            return 0

        lax.fori_loop(0, chips, arrive, 0)

    def finish_sends(which):
        st, pt, ct, ra, sb, rb, rx = refs(which)
        pair_copy(which).wait_send()
        relay_copy(which, chip).wait_send()

        def body(k, _):
            j = lax.rem(chip + k, chips)
            chip_copy("a", which, ct, ra, j, j, j).wait_send()
            chip_copy("b", which, sb, rb, j, j, j).wait_send()
            relay_copy(which, j).wait_send()
            return 0

        lax.fori_loop(1, chips, body, 0)

    def apply_carries(which, reads, h):
        pt, rx, oc = scratch["pt"].at[which], scratch["rx"].at[which], scratch["oc"]
        own_user = pt[0, share + 1 : share + 2, 0:1].astype(f32)
        other_user = rx[0, share : share + 1, 0:1].astype(f32)
        own = jnp.where(user_col == own_user, own_col[:, h : h + 1], 0.0)
        other = jnp.where(user_col == other_user, other_col[:, h : h + 1], 0.0)
        base = h * pieces
        if pieces == 1:
            state, far = oc[base], rx[base, 0:share, :]
        else:
            state = jnp.concatenate([oc[base + q] for q in range(pieces)], axis=0)
            far = jnp.concatenate([rx[base + q, 0:share, :] for q in range(pieces)], axis=0)
        return own * matmul(reads, state, 1, 0) + other * matmul(reads, far, 1, 0)

    get_feat.wait()
    make_states(0, feat, keys_t)
    both_rows = jnp.concatenate([keys_t[...], reads_t[...]], axis=0).astype(f32).T.astype(bf16)
    in_rows, out_rows = both_rows[:, 0:nstate], both_rows[:, nstate:]
    scores = matmul(out_rows, keys_t[...], 1, 0)
    scores = jnp.where(row_of == column_of, 2.0 * scores, scores)
    scores = jnp.where(user_col == user_row, scores, 0.0)
    send_chip(0)
    if fused:
        for k in range(1, count_a):
            source = lax.rem(a + k, count_a)
            z_copy(source, k, source).wait_recv()
        w_y.start()
        w_x.start()

    mixw, y = scratch["mixw"], scratch["y"]
    for h in range(heads):
        spread = jnp.abs(along[:, h : h + 1] - cumulative[h : h + 1, :])
        weights = (scores * jnp.exp(-spread)).astype(bf16)
        mixw[h] = weights
        cols = slice(h * width, (h + 1) * width)
        y[:, cols] = matmul(weights, feat[:, cols], 1, 0)
    if fused:

        @pl.when(c == 0)
        def _():
            w_y.wait_recv()

        @pl.when(c == 1)
        def _():
            w_x.wait_recv()

        w_on.start()
    silu, cot, normed, grad_mixed = (
        scratch["silu"],
        scratch["cot"],
        scratch["normed"],
        scratch["grad_mixed"],
    )
    get_gate.wait()
    gates = gate[...].astype(f32)
    silu[...] = gates / (1.0 + jnp.exp(-gates))
    scan_states(0)
    get_grad.wait()
    if fused:

        @pl.when(c == 0)
        def _():
            w_x.wait_recv()

        @pl.when(c == 1)
        def _():
            w_y.wait_recv()

        w_on.wait_recv()
        w_core.start()
    relay(0)
    if fused:
        w_core.wait_recv()
        whole = full[...].reshape(inner_dim, out_dim)
    else:
        get_weight.wait()
        whole = scratch["full"][...]
    scale = norm_gain[...].astype(f32)
    cot[...] = matmul(out_grad[...], whole, 1, 1) * scale
    for h in range(heads):
        cols = slice(h * width, (h + 1) * width)
        y[:, cols] = (y[:, cols] + apply_carries(0, out_rows, h)) * silu[:, cols]
    gated = y[...]
    multiplier = lax.rsqrt(jnp.mean(gated * gated, axis=1, keepdims=True) + eps)
    back = cot[...]
    slope = jnp.mean(back * gated, axis=1, keepdims=True) * multiplier * multiplier
    grad_mixed[...] = ((back - gated * slope) * multiplier * silu[...]).astype(bf16)
    make_states(1, grad_mixed, reads_t)

    normed[...] = (y[...] * multiplier * scale).astype(bf16)
    if fused:
        part = scratch["part"]
        rss, rrs = scratch["rss"], scratch["rrs"]
        part[...] = matmul(normed[...], out_grad[...], 0, 0).astype(bf16).reshape(part.shape)
        one, two, turn, three, four = (
            scratch[name] for name in ("one", "two", "turn", "three", "four")
        )

        def r_copy(source, target, slot, peer):
            return remote(source, target, rss.at[count_a + slot], rrs.at[count_a + slot], peer)

        r_core = r_copy(part.at[:, :, :, 1 - c], one, 0, core_peer)
        r_far = r_copy(one.at[1 - x, :, 1 - b], two.at[0], 1, first_peer)
        r_near = r_copy(one.at[1 - fx, :, 1 - fb], two.at[1], 2, first_peer)
        r_on = r_copy(turn, two.at[2], 3, second_peer)
        r_core.start()
    else:
        weight_grad[...] = matmul(normed[...], out_grad[...], 0, 0)
    send_chip(1)
    if fused:
        r_core.wait_recv()
        one[...] = (one[...].astype(f32) + part[:, :, :, c].astype(f32)).astype(bf16)
        r_far.start()
        r_near.start()

    for h in range(heads):
        cols = slice(h * width, (h + 1) * width)
        y[:, cols] = matmul(mixw[h], grad_mixed[:, cols], 0, 0)
    mixed[...] = matmul(normed[...], whole, 1, 0).astype(bf16)
    scan_states(1)
    if fused:
        r_far.wait_recv()
        turn[...] = (two[0].astype(f32) + one[fx, :, fb].astype(f32)).astype(bf16)
        r_on.start()
    relay(1)
    if fused:
        r_near.wait_recv()
        r_on.wait_recv()
        three[...] = (
            two[1].astype(f32) + two[2].astype(f32) + one[x, :, b].astype(f32)
        ).astype(bf16)

        def last_copy(k, source, target, to):
            return remote(
                three.at[source],
                four.at[target],
                rss.at[k],
                rrs.at[target],
                {"ctx": to * 4 + b * 2 + c},
            )

        for k in range(1, count_a):
            to = lax.rem(a + k, count_a)
            last_copy(k, to, a, to).start()
    for h in range(heads):
        cols = slice(h * width, (h + 1) * width)
        feature_grad[:, cols] = (y[:, cols] + apply_carries(1, in_rows, h)).astype(bf16)
    finish_sends(0)
    finish_sends(1)
    if fused:
        result = three[a].astype(f32)
        for k in range(1, count_a):
            source = lax.rem(a + k, count_a)
            last_copy(k, source, source, source).wait_recv()
            result = result + four[source].astype(f32)
        weight_grad[...] = result
        for k in range(1, count_a):
            to = lax.rem(a + k, count_a)
            last_copy(k, to, a, to).wait_send()
            z_copy(a, k, to).wait_send()
        for copy in (w_y, w_x, w_on, w_core, r_core, r_far, r_near, r_on):
            copy.wait_send()


def local(
    dp,
    n,
    features,
    gate_in,
    state_in,
    state_out,
    step_size,
    decay_rate,
    user_ids,
    norm_gain,
    out_weight,
    out_grad,
):
    tokens, inner_dim = features.shape[1:]
    heads = step_size.shape[1]
    width = inner_dim // heads
    nstate = state_in.shape[2]
    rows, out_dim = out_weight.shape
    fused = dp == 2 and n == 16 and rows % 16 == 0
    share = 2 * heads * nstate // n
    chips = n // 2
    states = pltpu.VMEM((2, chips, share + AUX, width), bf16)
    dma = pltpu.SemaphoreType.DMA
    scratch = dict(
        st=pltpu.VMEM((2, 2, chips, share + AUX, width), bf16),
        pt=states,
        ct=states,
        ra=states,
        sb=states,
        rb=states,
        rx=states,
        oc=pltpu.VMEM((chips, share, width), bf16),
        p_send=dma((2,)),
        p_recv=dma((2,)),
        a_send=dma((2, chips)),
        a_recv=dma((2, chips)),
        b_send=dma((2, chips)),
        b_recv=dma((2, chips)),
        x_send=dma((2, chips)),
        x_recv=dma((2, chips)),
        loads=dma((4,)),
        feat=pltpu.VMEM((tokens, inner_dim), bf16),
        gate=pltpu.VMEM((tokens, inner_dim), bf16),
        out_grad=pltpu.VMEM((tokens, out_dim), bf16),
        mixw=pltpu.VMEM((heads, tokens, tokens), bf16),
        y=pltpu.VMEM((tokens, inner_dim), f32),
        silu=pltpu.VMEM((tokens, inner_dim), f32),
        cot=pltpu.VMEM((tokens, inner_dim), f32),
        normed=pltpu.VMEM((tokens, inner_dim), bf16),
        grad_mixed=pltpu.VMEM((tokens, inner_dim), bf16),
    )
    if fused:
        count_a = n // 4
        sems = dma((count_a + 4,))
        quarter = (count_a, rows, out_dim)
        scratch.update(
            full=pltpu.VMEM((2, count_a, 2, 2, rows, out_dim), bf16),
            part=pltpu.VMEM((2, count_a, 2, 2, rows, out_dim), bf16),
            one=pltpu.VMEM((2, count_a, 2, rows, out_dim), bf16),
            two=pltpu.VMEM((3, *quarter), bf16),
            turn=pltpu.VMEM(quarter, bf16),
            three=pltpu.VMEM(quarter, bf16),
            four=pltpu.VMEM(quarter, bf16),
            wss=sems,
            wrs=sems,
            rss=sems,
            rrs=sems,
        )
        held = out_weight
    else:
        held = lax.all_gather(out_weight, ("dp", "ctx"), axis=0, tiled=True)
        scratch.update(full=pltpu.VMEM(held.shape, bf16))
    names = list(scratch)

    def body(*refs):
        kernel(n, fused, *refs[:13], dict(zip(names, refs[13:])))

    vmem = pl.BlockSpec(memory_space=pltpu.VMEM)
    smem = pl.BlockSpec(memory_space=pltpu.SMEM)
    hbm = pl.BlockSpec(memory_space=pltpu.HBM)
    mixed, feature_grad, weight_grad = pl.pallas_call(
        body,
        out_shape=(
            jax.ShapeDtypeStruct((tokens, out_dim), bf16),
            jax.ShapeDtypeStruct((tokens, inner_dim), bf16),
            jax.ShapeDtypeStruct(held.shape, f32),
        ),
        in_specs=[hbm, hbm, vmem, vmem, vmem, smem, vmem, vmem, hbm, hbm],
        out_specs=(vmem, vmem, vmem),
        scratch_shapes=list(scratch.values()),
        compiler_params=pltpu.CompilerParams(
            collective_id=0, has_side_effects=True, vmem_limit_bytes=62 << 20
        ),
        name="mixer",
    )(
        features[0],
        gate_in[0],
        state_in[0].T,
        state_out[0].T,
        step_size[0],
        decay_rate,
        user_ids,
        norm_gain.reshape(1, -1),
        held,
        out_grad[0],
    )
    if not fused:
        weight_grad = lax.psum_scatter(
            weight_grad, ("dp", "ctx"), scatter_dimension=0, tiled=True
        )
    return mixed[None], feature_grad[None], weight_grad


def solution(mesh):
    placed = (
        P("dp", "ctx", None),
        P("dp", "ctx", None),
        P("dp", "ctx", None),
        P("dp", "ctx", None),
        P("dp", None, "ctx"),
        P(),
        P("dp", "ctx"),
        P(),
        P(("dp", "ctx"), None),
        P("dp", "ctx", None),
    )
    return jax.shard_map(
        functools.partial(local, mesh.shape["dp"], mesh.shape["ctx"]),
        mesh=mesh,
        in_specs=placed,
        out_specs=(P("dp", "ctx", None), P("dp", "ctx", None), P(("dp", "ctx"), None)),
        check_vma=False,
    )
```

```python
import functools

import jax
import jax.numpy as jnp
from jax import lax
from jax.experimental import pallas as pl
from jax.experimental.pallas import tpu as pltpu
from jax.sharding import PartitionSpec as P

eps = 1e-05
MESH = pl.DeviceIdType.MESH
f32 = jnp.float32
bf16 = jnp.bfloat16
AUX = 16


def matmul(a, b, ca, cb, precision=None):
    return lax.dot_general(
        a, b, (((ca,), (cb,)), ((), ())), preferred_element_type=f32, precision=precision
    )


def kernel(
    n,
    fused,
    feat_hbm,
    gate_hbm,
    keys_t,
    reads_t,
    step,
    rate,
    users,
    norm_gain,
    weight_hbm,
    out_grad_hbm,
    mixed,
    feature_grad,
    weight_grad,
    scratch,
):
    me = lax.axis_index("ctx")
    x = lax.axis_index("dp")
    chips = n // 2
    chip, c = me // 2, me % 2
    feat, gate, out_grad = scratch["feat"], scratch["gate"], scratch["out_grad"]
    tokens, inner_dim = feat.shape
    heads = step.shape[0]
    width = inner_dim // heads
    nstate = keys_t.shape[0]
    share = 2 * heads * nstate // n
    pieces = nstate // share
    core_peer = {"ctx": chip * 2 + 1 - c}
    loads = scratch["loads"]

    def signal(to):
        pl.semaphore_signal(barrier, inc=1, device_id=to, device_id_type=MESH)

    def remote(source, target, send_sem, recv_sem, to):
        return pltpu.make_async_remote_copy(
            src_ref=source,
            dst_ref=target,
            send_sem=send_sem,
            recv_sem=recv_sem,
            device_id=to,
            device_id_type=MESH,
        )

    get_feat = pltpu.make_async_copy(feat_hbm, feat, loads.at[0])
    get_gate = pltpu.make_async_copy(gate_hbm, gate, loads.at[1])
    get_grad = pltpu.make_async_copy(out_grad_hbm, out_grad, loads.at[2])
    if fused:
        count_a = n // 4
        a, b = me // 4, (me // 2) % 2
        full, wss, wrs = scratch["full"], scratch["wss"], scratch["wrs"]
        rows, out_dim = weight_hbm.shape
        get_weight = pltpu.make_async_copy(weight_hbm, full.at[x, a, b, c], loads.at[3])
    else:
        get_weight = pltpu.make_async_copy(weight_hbm, scratch["full"], loads.at[3])
    get_weight.start()
    get_feat.start()
    get_grad.start()
    get_gate.start()

    barrier = pltpu.get_barrier_semaphore()

    def greet(k, _):
        signal({"ctx": lax.rem(chip + k, chips) * 2 + c})
        return 0

    lax.fori_loop(1, chips, greet, 0)
    signal(core_peer)
    if fused:
        signal({"dp": 1 - x})
    pl.semaphore_wait(barrier, chips + (1 if fused else 0))

    if fused:
        get_weight.wait()
        fx = x + c * (1 - 2 * x)
        fb = b + (1 - c) * (1 - 2 * b)
        y_peer = {"dp": x, "ctx": a * 4 + (1 - b) * 2 + c}
        x_peer = {"dp": 1 - x, "ctx": me}
        first_peer = {
            "dp": 1 - fx,
            "ctx": a * 4 + (1 - fb) * 2 + c,
        }
        second_peer = {"dp": fx, "ctx": a * 4 + fb * 2 + c}

        def z_copy(source, slot, to):
            view = full.at[x, source, b, c]
            return remote(
                view, view, wss.at[slot], wrs.at[source], {"ctx": to * 4 + b * 2 + c}
            )

        def w_copy(view, slot, peer):
            return remote(view, view, wss.at[count_a + slot], wrs.at[count_a + slot], peer)

        for k in range(1, count_a):
            z_copy(a, k, lax.rem(a + k, count_a)).start()
        w_y = w_copy(full.at[x, :, b, c], 0, y_peer)
        w_x = w_copy(full.at[x, :, b, c], 1, x_peer)
        w_on = w_copy(full.at[fx, :, fb, c], 2, first_peer)
        quarters = ((1 - x, 1 - b), (1 - x, b), (x, 1 - b), (x, b))
        w_core = [
            w_copy(full.at[i, :, j, c], 3 + slot, core_peer)
            for slot, (i, j) in enumerate(quarters)
        ]

    row_of = lax.broadcasted_iota(jnp.int32, (tokens, tokens), 0)
    column_of = lax.broadcasted_iota(jnp.int32, (tokens, tokens), 1)
    head_of = lax.broadcasted_iota(jnp.int32, (heads, 1), 0)
    rates = jnp.zeros((heads, 1), f32)
    for h in range(heads):
        rates = jnp.where(head_of == h, rate[h], rates)
    logdec = -step[...] * rates
    upto = (row_of <= column_of).astype(f32)
    cumulative = matmul(logdec, upto, 1, 0, lax.Precision.HIGHEST)
    total = cumulative[:, tokens - 1 : tokens]
    user_row = users[...].astype(f32)
    first_user = user_row[:, 0:1]
    last_user = user_row[:, tokens - 1 : tokens]
    from_start = jnp.exp(cumulative)
    to_end = jnp.exp(total - cumulative)
    passing = jnp.exp(total)
    fwd_scale = jnp.where(user_row == last_user, to_end, 0.0)
    rev_scale = jnp.where(user_row == first_user, from_start, 0.0)
    stacked = jnp.concatenate(
        [
            cumulative,
            from_start,
            to_end,
            jnp.broadcast_to(user_row, (8, tokens)),
            jnp.zeros((tokens - 3 * heads - 8, tokens), f32),
        ],
        axis=0,
    ).T
    along = stacked[:, 0:heads]
    start_col = stacked[:, heads : 2 * heads]
    end_col = stacked[:, 2 * heads : 3 * heads]
    user_col = stacked[:, 3 * heads : 3 * heads + 1]
    own_col = jnp.where(c == 1, start_col, end_col)
    other_col = jnp.where(c == 1, end_col, start_col)
    aux_row = lax.broadcasted_iota(jnp.int32, (AUX, width), 0)

    def chip_copy(name, which, source, target, index, slot, to):
        return remote(
            source.at[index],
            target.at[slot],
            scratch[name + "_send"].at[which, to],
            scratch[name + "_recv"].at[which, slot],
            {"ctx": to * 2 + c},
        )

    def refs(which):
        return [scratch[name].at[which] for name in ("st", "pt", "ct", "ra", "sb", "rb", "rx")]

    def pair_copy(which):
        st, pt = refs(which)[:2]
        return remote(
            st.at[c], pt, scratch["p_send"].at[which], scratch["p_recv"].at[which], core_peer
        )

    def relay_copy(which, u):
        rb, rx = refs(which)[5:]
        return remote(
            rb.at[u],
            rx.at[u],
            scratch["x_send"].at[which, u],
            scratch["x_recv"].at[which, u],
            core_peer,
        )

    def make_states(which, values, keys):
        st = refs(which)[0]
        wide = keys[...].astype(f32)
        for h in range(heads):
            v = values[:, h * width : (h + 1) * width]
            both = jnp.concatenate(
                [wide * fwd_scale[h : h + 1, :], wide * rev_scale[h : h + 1, :]], axis=0
            ).astype(bf16)
            states = matmul(both, v, 1, 0).astype(bf16)
            for d in range(2):
                aux = jnp.where(
                    aux_row == 0, passing[h : h + 1, :], last_user if d == 0 else first_user
                ).astype(bf16)
                for q in range(pieces):
                    start = d * nstate + q * share
                    st[d, h * pieces + q, 0:share, :] = states[start : start + share]
                    st[d, h * pieces + q, share : share + AUX, :] = aux
        pair_copy(which).start()

    def send_chip(which):
        st, pt, ct, ra, sb, rb, rx = refs(which)
        pair_copy(which).wait_recv()
        mine, theirs = st[1 - c].astype(f32), pt[...].astype(f32)
        gain = mine[:, share : share + 1]
        same = mine[:, share + 1 : share + 2] == theirs[:, share + 1 : share + 2]
        ct[:, 0:share, :] = (
            jnp.where(same, gain, 0.0) * theirs[:, 0:share] + mine[:, 0:share]
        ).astype(bf16)
        ct[:, share : share + AUX, :] = jnp.where(
            aux_row[None] == 0, mine[:, share:] * theirs[:, share:], mine[:, share:]
        ).astype(bf16)

        def send(k, _):
            to = lax.rem(chip + k, chips)
            chip_copy("a", which, ct, ra, to, chip, to).start()
            return 0

        lax.fori_loop(1, chips, send, 0)
        ra[chip] = ct[chip]

    def scan_states(which):
        st, pt, ct, ra, sb, rb, rx = refs(which)

        def body(p, carry):
            running, previous = carry
            j = p + (1 - c) * (chips - 1 - 2 * p)

            @pl.when(j != chip)
            def _():
                chip_copy("a", which, ct, ra, j, j, j).wait_recv()

            sb[j, 0:share, :] = running.astype(bf16)
            sb[j, share : share + AUX, :] = jnp.broadcast_to(previous, (AUX, width)).astype(bf16)

            @pl.when(j != chip)
            def _():
                chip_copy("b", which, sb, rb, j, chip, j).start()

            block = ra[j].astype(f32)
            boundary = block[share + 1 : share + 2]
            gain = jnp.where(boundary == previous, block[share : share + 1], 0.0)
            running = (gain * running + block[0:share]).astype(bf16).astype(f32)
            return running, boundary

        lax.fori_loop(
            0, chips, body, (jnp.zeros((share, width), f32), jnp.full((1, width), -1.0, f32))
        )
        rb[chip] = sb[chip]
        relay_copy(which, chip).start()

    def relay(which):
        st, pt, ct, ra, sb, rb, rx = refs(which)

        def body(k, _):
            u = lax.rem(chip + k, chips)
            chip_copy("b", which, sb, rb, u, u, u).wait_recv()
            relay_copy(which, u).start()
            return 0

        lax.fori_loop(1, chips, body, 0)
        theirs, past = pt[...].astype(f32), rb[...].astype(f32)
        same = theirs[:, share + 1 : share + 2] == past[:, share + 1 : share + 2]
        scratch["oc"][...] = (
            jnp.where(same, theirs[:, share : share + 1], 0.0) * past[:, 0:share]
            + theirs[:, 0:share]
        ).astype(bf16)

        def arrive(u, _):
            relay_copy(which, u).wait_recv()
            return 0

        lax.fori_loop(0, chips, arrive, 0)

    def finish_sends(which):
        st, pt, ct, ra, sb, rb, rx = refs(which)
        pair_copy(which).wait_send()
        relay_copy(which, chip).wait_send()

        def body(k, _):
            j = lax.rem(chip + k, chips)
            chip_copy("a", which, ct, ra, j, j, j).wait_send()
            chip_copy("b", which, sb, rb, j, j, j).wait_send()
            relay_copy(which, j).wait_send()
            return 0

        lax.fori_loop(1, chips, body, 0)

    def apply_carries(which, reads, h):
        pt, rx, oc = scratch["pt"].at[which], scratch["rx"].at[which], scratch["oc"]
        own_user = pt[0, share + 1 : share + 2, 0:1].astype(f32)
        other_user = rx[0, share : share + 1, 0:1].astype(f32)
        own = jnp.where(user_col == own_user, own_col[:, h : h + 1], 0.0)
        other = jnp.where(user_col == other_user, other_col[:, h : h + 1], 0.0)
        base = h * pieces
        if pieces == 1:
            state, far = oc[base], rx[base, 0:share, :]
        else:
            state = jnp.concatenate([oc[base + q] for q in range(pieces)], axis=0)
            far = jnp.concatenate([rx[base + q, 0:share, :] for q in range(pieces)], axis=0)
        return own * matmul(reads, state, 1, 0) + other * matmul(reads, far, 1, 0)

    get_feat.wait()
    make_states(0, feat, keys_t)
    both_rows = jnp.concatenate([keys_t[...], reads_t[...]], axis=0).astype(f32).T.astype(bf16)
    in_rows, out_rows = both_rows[:, 0:nstate], both_rows[:, nstate:]
    scores = matmul(out_rows, keys_t[...], 1, 0)
    scores = jnp.where(row_of == column_of, 2.0 * scores, scores)
    scores = jnp.where(user_col == user_row, scores, 0.0)
    send_chip(0)
    if fused:
        for k in range(1, count_a):
            source = lax.rem(a + k, count_a)
            z_copy(source, k, source).wait_recv()
        w_y.start()
        w_x.start()
        w_core[3].start()

    mixw, y = scratch["mixw"], scratch["y"]
    for h in range(heads):
        spread = jnp.abs(along[:, h : h + 1] - cumulative[h : h + 1, :])
        weights = (scores * jnp.exp(-spread)).astype(bf16)
        mixw[h] = weights
        cols = slice(h * width, (h + 1) * width)
        y[:, cols] = matmul(weights, feat[:, cols], 1, 0)
    if fused:

        @pl.when(c == 0)
        def _():
            w_y.wait_recv()
            w_on.start()
            w_core[2].start()

        @pl.when(c == 1)
        def _():
            w_x.wait_recv()
            w_on.start()
            w_core[1].start()

    silu, cot, normed, grad_mixed = (
        scratch["silu"],
        scratch["cot"],
        scratch["normed"],
        scratch["grad_mixed"],
    )
    get_gate.wait()
    gates = gate[...].astype(f32)
    silu[...] = gates / (1.0 + jnp.exp(-gates))
    scan_states(0)
    get_grad.wait()
    if fused:

        @pl.when(c == 0)
        def _():
            w_x.wait_recv()
            w_core[1].start()

        @pl.when(c == 1)
        def _():
            w_y.wait_recv()
            w_core[2].start()

        w_on.wait_recv()
        w_core[0].start()
    relay(0)
    if fused:
        for copy in w_core:
            copy.wait_recv()
        whole = full[...].reshape(inner_dim, out_dim)
    else:
        get_weight.wait()
        whole = scratch["full"][...]
    scale = norm_gain[...].astype(f32).reshape(1, -1)
    cot[...] = matmul(out_grad[...], whole, 1, 1) * scale
    for h in range(heads):
        cols = slice(h * width, (h + 1) * width)
        y[:, cols] = (y[:, cols] + apply_carries(0, out_rows, h)) * silu[:, cols]
    gated = y[...]
    multiplier = lax.rsqrt(jnp.mean(gated * gated, axis=1, keepdims=True) + eps)
    back = cot[...]
    slope = jnp.mean(back * gated, axis=1, keepdims=True) * multiplier * multiplier
    grad_mixed[...] = ((back - gated * slope) * multiplier * silu[...]).astype(bf16)
    make_states(1, grad_mixed, reads_t)

    normed[...] = (y[...] * multiplier * scale).astype(bf16)
    if fused:
        part = scratch["part"]
        rss, rrs = scratch["rss"], scratch["rrs"]
        part[...] = matmul(normed[...], out_grad[...], 0, 0).astype(bf16).reshape(part.shape)
        one, two, turn, three, four = (
            scratch[name] for name in ("one", "two", "turn", "three", "four")
        )

        def r_copy(source, target, slot, peer):
            return remote(source, target, rss.at[count_a + slot], rrs.at[count_a + slot], peer)

        r_core = [
            r_copy(part.at[i, :, j, 1 - c], one.at[i, :, j], slot, core_peer)
            for slot, (i, j) in enumerate(quarters)
        ]
        r_far = r_copy(one.at[1 - x, :, 1 - b], two.at[0], 4, first_peer)
        r_near = r_copy(one.at[1 - fx, :, 1 - fb], two.at[1], 5, first_peer)
        r_on = r_copy(turn, two.at[2], 6, second_peer)
        for copy in r_core:
            copy.start()
    else:
        weight_grad[...] = matmul(normed[...], out_grad[...], 0, 0)
    send_chip(1)
    if fused:
        for slot, (i, j) in enumerate(quarters):
            r_core[slot].wait_recv()
            one[i, :, j] = (one[i, :, j].astype(f32) + part[i, :, j, c].astype(f32)).astype(bf16)
            if slot == 0:
                r_far.start()
            if slot == 2:
                r_near.start()

    for h in range(heads):
        cols = slice(h * width, (h + 1) * width)
        y[:, cols] = matmul(mixw[h], grad_mixed[:, cols], 0, 0)
    mixed[...] = matmul(normed[...], whole, 1, 0).astype(bf16)
    scan_states(1)
    if fused:
        r_far.wait_recv()
        turn[...] = (two[0].astype(f32) + one[fx, :, fb].astype(f32)).astype(bf16)
        r_on.start()
    relay(1)
    if fused:
        r_near.wait_recv()
        r_on.wait_recv()
        three[...] = (
            two[1].astype(f32) + two[2].astype(f32) + one[x, :, b].astype(f32)
        ).astype(bf16)

        def last_copy(k, source, target, to):
            return remote(
                three.at[source],
                four.at[target],
                rss.at[k],
                rrs.at[target],
                {"ctx": to * 4 + b * 2 + c},
            )

        for k in range(1, count_a):
            to = lax.rem(a + k, count_a)
            last_copy(k, to, a, to).start()
    for h in range(heads):
        cols = slice(h * width, (h + 1) * width)
        feature_grad[:, cols] = (y[:, cols] + apply_carries(1, in_rows, h)).astype(bf16)
    finish_sends(0)
    finish_sends(1)
    if fused:
        result = three[a].astype(f32)
        for k in range(1, count_a):
            source = lax.rem(a + k, count_a)
            last_copy(k, source, source, source).wait_recv()
            result = result + four[source].astype(f32)
        weight_grad[...] = result
        for k in range(1, count_a):
            to = lax.rem(a + k, count_a)
            last_copy(k, to, a, to).wait_send()
            z_copy(a, k, to).wait_send()
        for copy in (w_y, w_x, w_on, r_far, r_near, r_on, *w_core, *r_core):
            copy.wait_send()


def local(
    dp,
    n,
    features,
    gate_in,
    state_in,
    state_out,
    step_size,
    decay_rate,
    user_ids,
    norm_gain,
    out_weight,
    out_grad,
):
    tokens, inner_dim = features.shape[1:]
    heads = step_size.shape[1]
    width = inner_dim // heads
    nstate = state_in.shape[2]
    rows, out_dim = out_weight.shape
    fused = dp == 2 and n == 16 and rows % 16 == 0
    share = 2 * heads * nstate // n
    chips = n // 2
    states = pltpu.VMEM((2, chips, share + AUX, width), bf16)
    dma = pltpu.SemaphoreType.DMA
    scratch = dict(
        st=pltpu.VMEM((2, 2, chips, share + AUX, width), bf16),
        pt=states,
        ct=states,
        ra=states,
        sb=states,
        rb=states,
        rx=states,
        oc=pltpu.VMEM((chips, share, width), bf16),
        p_send=dma((2,)),
        p_recv=dma((2,)),
        a_send=dma((2, chips)),
        a_recv=dma((2, chips)),
        b_send=dma((2, chips)),
        b_recv=dma((2, chips)),
        x_send=dma((2, chips)),
        x_recv=dma((2, chips)),
        loads=dma((4,)),
        feat=pltpu.VMEM((tokens, inner_dim), bf16),
        gate=pltpu.VMEM((tokens, inner_dim), bf16),
        out_grad=pltpu.VMEM((tokens, out_dim), bf16),
        mixw=pltpu.VMEM((heads, tokens, tokens), bf16),
        y=pltpu.VMEM((tokens, inner_dim), f32),
        silu=pltpu.VMEM((tokens, inner_dim), f32),
        cot=pltpu.VMEM((tokens, inner_dim), f32),
        normed=pltpu.VMEM((tokens, inner_dim), bf16),
        grad_mixed=pltpu.VMEM((tokens, inner_dim), bf16),
    )
    if fused:
        count_a = n // 4
        sems = dma((count_a + 7,))
        quarter = (count_a, rows, out_dim)
        scratch.update(
            full=pltpu.VMEM((2, count_a, 2, 2, rows, out_dim), bf16),
            part=pltpu.VMEM((2, count_a, 2, 2, rows, out_dim), bf16),
            one=pltpu.VMEM((2, count_a, 2, rows, out_dim), bf16),
            two=pltpu.VMEM((3, *quarter), bf16),
            turn=pltpu.VMEM(quarter, bf16),
            three=pltpu.VMEM(quarter, bf16),
            four=pltpu.VMEM(quarter, bf16),
            wss=sems,
            wrs=sems,
            rss=sems,
            rrs=sems,
        )
        held = out_weight
    else:
        held = lax.all_gather(out_weight, ("dp", "ctx"), axis=0, tiled=True)
        scratch.update(full=pltpu.VMEM(held.shape, bf16))
    names = list(scratch)

    def body(*refs):
        kernel(n, fused, *refs[:13], dict(zip(names, refs[13:])))

    vmem = pl.BlockSpec(memory_space=pltpu.VMEM)
    smem = pl.BlockSpec(memory_space=pltpu.SMEM)
    hbm = pl.BlockSpec(memory_space=pltpu.HBM)
    mixed, feature_grad, weight_grad = pl.pallas_call(
        body,
        out_shape=(
            jax.ShapeDtypeStruct((tokens, out_dim), bf16),
            jax.ShapeDtypeStruct((tokens, inner_dim), bf16),
            jax.ShapeDtypeStruct(held.shape, f32),
        ),
        in_specs=[hbm, hbm, vmem, vmem, vmem, smem, vmem, vmem, hbm, hbm],
        out_specs=(vmem, vmem, vmem),
        scratch_shapes=list(scratch.values()),
        compiler_params=pltpu.CompilerParams(
            collective_id=0, has_side_effects=True, vmem_limit_bytes=62 << 20
        ),
        name="mixer",
    )(
        features[0],
        gate_in[0],
        state_in[0].T,
        state_out[0].T,
        step_size[0],
        decay_rate,
        user_ids,
        norm_gain,
        held,
        out_grad[0],
    )
    if not fused:
        weight_grad = lax.psum_scatter(
            weight_grad, ("dp", "ctx"), scatter_dimension=0, tiled=True
        )
    return mixed[None], feature_grad[None], weight_grad


def solution(mesh):
    placed = (
        P("dp", "ctx", None),
        P("dp", "ctx", None),
        P("dp", "ctx", None),
        P("dp", "ctx", None),
        P("dp", None, "ctx"),
        P(),
        P("dp", "ctx"),
        P(),
        P(("dp", "ctx"), None),
        P("dp", "ctx", None),
    )
    return jax.shard_map(
        functools.partial(local, mesh.shape["dp"], mesh.shape["ctx"]),
        mesh=mesh,
        in_specs=placed,
        out_specs=(P("dp", "ctx", None), P("dp", "ctx", None), P(("dp", "ctx"), None)),
        check_vma=False,
    )
```
